32 devices in a mesh: dp: 16 (over z, y, x), vocab: 2 (over core).
Axes of the slice: x: 2, y: 2, z: 4, core: 2. Of those that a mesh axis runs over, the one named last changes fastest.
Arguments:
- tokens: int32 [144, 512], P('dp'), may hold values from 0 to 32127
- span_bounds: int32 [144, 16, 2], P('dp'), may hold values from 1 to 512, as said below
- owner: int32 [144, 80, 1], P('dp'), may hold values from 0 to 15; in each aligned block of 720 rows (0 to 719, 720 to 1439, ..., all dimensions but the last counted through in order) at most 48 rows name the same one
- decoder_states: bfloat16 [144, 80, 1024], P('dp', None, 'vocab'), may hold values from -1024 to 1024
- norm_gain: bfloat16 [1024], replicated, may hold values from 0.25 to 1.75
- embedding: bfloat16 [32128, 1024], P('vocab', 'dp'), may hold values from -64 to 64
Outputs:
- losses: float32 [12288], P('dp')
The draws below stay inside these ranges and needn't reach their ends.
Inputs may be any that keep to these rules, and one draw needn't show every extreme that they name: `span_bounds`: within a sequence the 16 spans are disjoint and in increasing order, each with span_end - span_start from 1 to 5; every sequence has a span of exactly 5. Among the slots of one dp device no owner is named more than 48 times; in some of those blocks an owner is named exactly 48 times.
All inputs are finite; a program needn't handle non-finite values.
Results may differ from the reference program's by a relative error of at most 0.00047.
Values may be sent and summed in bfloat16 or wider, within the bound.
A program may use at most 128 MiB of HBM per device.

```python
import math
import jax
import jax.numpy as jnp
import numpy as np
from jax import lax

D = 1024
VOCAB = 32128
LEN = 512
NSPAN = 16
MAXSPAN = 5
SEQ_DEV = 9
SEQS = 144
OWN_ROWS = 768
CAP = 48
N_DP = 16


def draw_span_bounds(key, part):
    key_len, key_long, key_gap = jax.random.split(jax.random.fold_in(key, 11), 3)
    lengths = jax.random.randint(key_len, (SEQS, NSPAN), 1, MAXSPAN + 1)
    longest = jax.random.randint(key_long, (SEQS, 1), 0, NSPAN)
    lengths = jnp.where(jnp.arange(NSPAN)[None, :] == longest, MAXSPAN, lengths)
    spacing = jax.random.randint(key_gap, (SEQS, NSPAN), 1, LEN // NSPAN - MAXSPAN + 1)
    span_ends = jnp.cumsum(spacing + lengths, axis=1)
    shifted = span_ends + (LEN - span_ends[:, -1:])
    starts = shifted - lengths
    return jnp.stack([starts, shifted], axis=-1).astype(jnp.int32)


def shared_patterns(key):
    key_col, key_topic, key_lead = jax.random.split(jax.random.fold_in(key, 7), 3)
    topic_count = max(4, min(32, VOCAB // 1000))
    col_scale = jnp.exp(jax.random.uniform(key_col, (D,), jnp.float32, math.log(0.5), math.log(2.0)))
    col_scale = col_scale / jnp.sqrt(jnp.mean(col_scale * col_scale))
    raw = jax.random.normal(key_topic, (topic_count, D), jnp.float32) / col_scale[None, :]
    topics = raw / jnp.sqrt(jnp.sum(raw * raw, axis=1, keepdims=True))
    pattern = 102.4 / math.sqrt(D) * jnp.clip(jax.random.normal(key_lead, (8, D), jnp.float32), -1.4, 1.4)
    leading = pattern * jnp.linspace(1.4, 3.8, 8).astype(jnp.float32)[:, None]
    return (col_scale, topics, leading)


def draw_embedding(key, part):
    col_scale, topics, leading = shared_patterns(key)
    key_perm, key_base, key_row, key_strength, key_noise = jax.random.split(jax.random.fold_in(key, 31), 5)
    topic_count = topics.shape[0]
    heavy_count = max(4, VOCAB // 64)
    order = jax.random.permutation(key_perm, VOCAB)
    leading_rows = order[:8]
    runner_rows = order[8:16]
    topic_rows = order[16:16 + heavy_count]
    row_scale = jnp.exp(jax.random.uniform(key_row, (VOCAB, 1), jnp.float32, 0.0, math.log(4.0)))
    vocab_table = 1.5 * jnp.clip(jax.random.normal(key_base, (VOCAB, D), jnp.float32), -4.0, 4.0) * row_scale * col_scale[None, :]
    strength = jax.random.uniform(key_strength, (heavy_count, 1), jnp.float32, 2.0, 3.2) * math.log(VOCAB)
    topic_ids = jnp.arange(heavy_count) % topic_count
    vocab_table = vocab_table.at[topic_rows].add(strength * topics[topic_ids])
    length = jnp.sqrt(jnp.sum(leading * leading, axis=1, keepdims=True))
    runner = jnp.clip(leading - 2.0 * leading / length + 0.3 * jax.random.normal(key_noise, (8, D), jnp.float32), -64.0, 64.0)
    vocab_table = vocab_table.at[leading_rows].set(leading).at[runner_rows].set(runner)
    return jnp.clip(vocab_table, -64.0, 64.0).astype(jnp.bfloat16)


def draw_decoder_states(key, part):
    col_scale, topics, leading = shared_patterns(key)
    key_row = jax.random.fold_in(jax.random.fold_in(key, 23), 0)
    key_col = jax.random.fold_in(jax.random.fold_in(key, 23), 1)
    key_body = jax.random.fold_in(jax.random.fold_in(key, 23), 3)
    key_pick = jax.random.fold_in(jax.random.fold_in(key, 23), 4)
    key_which = jax.random.fold_in(jax.random.fold_in(key, 23), 5)
    key_topic = jax.random.fold_in(jax.random.fold_in(key, 23), 6)
    key_cos = jax.random.fold_in(jax.random.fold_in(key, 23), 7)
    slot_count = NSPAN * MAXSPAN
    shape = (SEQS, slot_count, D)
    row_scale = jnp.exp(jax.random.uniform(key_row, (SEQS, slot_count, 1), jnp.float32, 0.0, math.log(10.0)))
    state_cols = jnp.exp(jax.random.uniform(key_col, (D,), jnp.float32, 0.0, math.log(10.0)))
    noise = jnp.clip(jax.random.normal(key_body, shape, jnp.float32), -4.0, 4.0) * state_cols
    noise = noise / jnp.sqrt(jnp.sum(noise * noise, axis=2, keepdims=True))
    topic_pick = jax.random.randint(key_topic, (SEQS, slot_count), 0, topics.shape[0])
    cosine = jax.random.uniform(key_cos, (SEQS, slot_count, 1), jnp.float32, 0.5, 0.85)
    direction = cosine * topics[topic_pick] + jnp.sqrt(1.0 - cosine * cosine) * noise
    states = direction * math.sqrt(D) * row_scale
    forced = (jnp.arange(SEQS)[:, None] == 0) & (jnp.arange(slot_count)[None, :] == 0)
    picked = jax.random.bernoulli(key_pick, 0.005, (SEQS, slot_count)) | forced
    which = jax.random.randint(key_which, (SEQS, slot_count), 0, 8)
    aligned = leading[which] * row_scale * 0.25
    states = jnp.where(picked[:, :, None], aligned, states)
    return jnp.clip(states, -1024.0, 1024.0).astype(jnp.bfloat16)


def touch_ends(values, key, smallest, high):
    longest = values.shape.index(max(values.shape))
    spots = []
    for shift in (0, 1):
        where = [jax.random.randint(jax.random.fold_in(key, axis), (), 0, length) for axis, length in enumerate(values.shape)]
        where[longest] = (where[longest] + shift) % values.shape[longest]
        spots.append(tuple(where))
    return values.at[spots[0]].set(smallest).at[spots[1]].set(high)


def rank_table(count, lean):
    weights = [(1 << 20) // math.isqrt(grade ** lean) + 1 for grade in range(1, count + 1)]
    scale = 1 + sum(weights) // (1 << 30)
    return np.cumsum(np.array([max(1, weight // scale) for weight in weights]))


def ranked(stream_key, extent, amount, slope):
    listing = rank_table(amount, slope)
    ticket = jax.random.randint(jax.random.fold_in(stream_key, 1), extent, 0, int(listing[amount - 1]))
    standing = jnp.searchsorted(jnp.asarray(listing, jnp.int32), ticket, side="right")
    return jax.random.permutation(jax.random.fold_in(stream_key, 2), amount)[standing].astype(jnp.int32)


def routed_block(key, own, number, rows, amount, top, reach, lean):
    ranking = jax.random.permutation(key, amount)
    heavy_load, usual = portions_of(amount, rows * top, reach, lean, True), portions_of(amount, rows * top, reach, lean, False)
    places = jnp.arange(amount)

    def named(sizes, rotation):
        used = int((sizes > 0).sum())
        fixed = max(1, used // 4)
        passed = fixed + (places - fixed + rotation * (used - fixed)) % max(1, amount - fixed)
        return jnp.zeros((amount,), jnp.int32).at[ranking[jnp.where(places < fixed, places, passed)]].set(jnp.asarray(sizes, jnp.int32))

    sizes = jnp.where(number % 4 == 0, named(heavy_load, number // 4), named(usual, number - number // 4 - 1))
    mixed = jax.random.permutation(jax.random.fold_in(own, 3), amount)
    donor, receiver = mixed[0:amount // 2 * 2:2], mixed[1:amount // 2 * 2:2]
    room = jnp.minimum(sizes[donor] - 1, reach - sizes[receiver]) // 2
    room = jnp.where((donor == ranking[0]) | (receiver == ranking[0]) | (sizes[receiver] == 0), 0, jnp.maximum(room, 0))
    passed = jax.random.randint(jax.random.fold_in(own, 4), (amount // 2,), 0, 1 << 20) % (room + 1)
    sizes = sizes.at[donor].add(-passed).at[receiver].add(passed)
    items = jnp.searchsorted(jnp.cumsum(sizes), jnp.arange(rows * top), side="right").astype(jnp.int32)
    grid = items.reshape(top, rows).T
    grid = grid[jax.random.permutation(jax.random.fold_in(own, 1), rows)]
    rotation = jax.random.randint(jax.random.fold_in(own, 2), (rows, 1), 0, top)
    return jnp.take_along_axis(grid, (jnp.arange(top)[None, :] + rotation) % top, axis=1)


def portions_of(count, total, most, slope, full):
    loads = [(1 << 20) // math.isqrt(rank ** slope) + 1 for rank in range(1, count + 1)]
    largest = most if full else min(most, max(-(-total // count), total * loads[0] // sum(loads)))
    least = 1 if total - largest >= count - 1 else 0
    counts, surplus = [largest] + [least] * (count - 1), total - largest - least * (count - 1)
    while surplus > 0:
        movable = [i for i in range(1, count) if counts[i] < largest] or [i for i in range(1, count) if counts[i] < most]
        whole, left = sum([loads[i] for i in movable]), surplus
        for i in movable:
            extra = min(most - counts[i], max(1, left * loads[i] // whole), surplus)
            counts[i] = counts[i] + extra
            surplus = surplus - extra
    return np.array(counts)


def setup_inputs(seed: int = 0) -> dict:
    streams_of = jax.random.split(jax.random.key(seed), 7)
    tokens = touch_ends(ranked(streams_of[0], (SEQS, LEN), VOCAB, 2), jax.random.fold_in(streams_of[0], 3), 0, VOCAB - 1).astype(jnp.int32)
    span_bounds = draw_span_bounds(jax.random.fold_in(streams_of[6], 71), 0)
    owner_keys = jax.random.split(jax.random.fold_in(streams_of[2], 1), SEQS * (NSPAN * MAXSPAN) // (SEQ_DEV * NSPAN * MAXSPAN))
    owner_turns = jax.random.permutation(jax.random.fold_in(streams_of[2], 3), SEQS * (NSPAN * MAXSPAN) // (SEQ_DEV * NSPAN * MAXSPAN))
    owner = jax.vmap(lambda own, number: routed_block(jax.random.fold_in(streams_of[2], 2), own, number, SEQ_DEV * NSPAN * MAXSPAN, N_DP, 1, CAP, 2))(owner_keys, owner_turns).reshape((SEQS, NSPAN * MAXSPAN, 1))
    decoder_states = draw_decoder_states(jax.random.fold_in(streams_of[6], 71), 0)
    norm_gain = jnp.clip(1.0 + 0.15 * jax.random.normal(streams_of[4], (D,), jnp.float32), 0.25, 1.75).astype(jnp.bfloat16)
    embedding = draw_embedding(jax.random.fold_in(streams_of[6], 71), 0)
    return dict(tokens=tokens, span_bounds=span_bounds, owner=owner, decoder_states=decoder_states, norm_gain=norm_gain, embedding=embedding)


epsilon = 1e-06

def reference(tokens, span_bounds, owner, decoder_states, norm_gain, embedding):
    slot_count = NSPAN * MAXSPAN
    slot_ids = jnp.arange(slot_count, dtype=jnp.int32)
    offsets = slot_ids % MAXSPAN
    starts = jnp.repeat(span_bounds[:, :, 0], MAXSPAN, axis=1)
    span_ends = jnp.repeat(span_bounds[:, :, 1], MAXSPAN, axis=1)
    is_live = offsets[None, :] < span_ends - starts
    positions = jnp.minimum(starts + offsets[None, :], LEN - 1).astype(jnp.int32)
    labels = jnp.take_along_axis(tokens, positions, axis=1)
    device_slots = SEQ_DEV * slot_count
    targets = owner.reshape(N_DP, device_slots)
    owner_hits = (targets[:, :, None] == jnp.arange(N_DP, dtype=jnp.int32)[None, None, :]).astype(jnp.int32)
    running = jnp.cumsum(owner_hits, axis=1) - owner_hits
    slot_rank = lax.optimization_barrier(jnp.sum(running * owner_hits, axis=2)).astype(jnp.int32)
    source = jnp.arange(N_DP, dtype=jnp.int32)[:, None]
    target_row = (targets * OWN_ROWS + source * CAP + slot_rank).astype(jnp.int32)
    states = decoder_states.reshape(N_DP, device_slots, D).astype(jnp.float32)
    mean_square = lax.optimization_barrier(jnp.mean(states * states, axis=2, keepdims=True))
    normed = (states * lax.rsqrt(mean_square + epsilon) * norm_gain.astype(jnp.float32) * D ** (-0.5)).astype(jnp.bfloat16)

    def device_loss(operands):
        row_block, row_labels = operands
        logits = lax.dot_general(row_block, embedding, (((1,), (1,)), ((), ())), preferred_element_type=jnp.float32)
        row_top = lax.optimization_barrier(jnp.max(logits, axis=1))
        exp_total = lax.optimization_barrier(jnp.sum(jnp.exp(logits - row_top[:, None]), axis=1))
        label_logit = jnp.take_along_axis(logits, row_labels[:, None].astype(jnp.int32), axis=1)[:, 0]
        return row_top + jnp.log(exp_total) - label_logit
    row_loss = lax.map(device_loss, (normed, labels.reshape(N_DP, device_slots)))
    live_flat = is_live.reshape(-1)
    slot_index = jnp.where(live_flat, target_row.reshape(-1), N_DP * OWN_ROWS).astype(jnp.int32)
    result = jnp.zeros((N_DP * OWN_ROWS,), jnp.float32)
    return result.at[slot_index].set(jnp.where(live_flat, row_loss.reshape(-1), 0.0).astype(jnp.float32), mode='drop')
```

```python
import functools

import jax
import jax.numpy as jnp
from jax import lax
from jax.experimental import pallas as pl
from jax.experimental.pallas import tpu as pltpu
from jax.sharding import PartitionSpec as P

MAXSPAN = 5
OWN_ROWS = 768
INNER = 4
LANES = 128
LOW = -1e30
MESH = pl.DeviceIdType.MESH


epsilon = 1e-06


def normalize(rows, norm_gain):
    values = rows.astype(jnp.float32)
    mean_square = jnp.mean(values * values, axis=1, keepdims=True)
    scaled = (
        values
        * lax.rsqrt(mean_square + epsilon)
        * norm_gain.astype(jnp.float32)
        * values.shape[1] ** (-0.5)
    )
    return scaled.astype(jnp.bfloat16)


def exchange_kernel(
    outer,
    inner,
    cores,
    chunk,
    rows_ref,
    labels_ref,
    table_ref,
    rows_out,
    labels_out,
    table_out,
    local_sem,
    table_send,
    table_recv,
    plane_send,
    plane_recv,
    rows_send,
    rows_recv,
    core_send,
    core_recv,
    label_send,
    label_recv,
):
    dp = lax.axis_index("dp")
    core = lax.axis_index("vocab")
    a = dp // inner
    b = lax.rem(dp, inner)

    def column(d):
        return (lax.rem(a + d, outer) * inner + b, core)

    def plane(e):
        return (a * inner + lax.rem(b + e, inner), core)

    def partner(f):
        return (dp, lax.rem(core + f, cores))

    barrier = pltpu.get_barrier_semaphore()
    greeted = (
        [column(d) for d in range(1, outer)]
        + [plane(e) for e in range(1, inner)]
        + [partner(f) for f in range(1, cores)]
    )
    for device in greeted:
        pl.semaphore_signal(barrier, inc=1, device_id=device, device_id_type=MESH)
    pl.semaphore_wait(barrier, len(greeted))

    def table_piece(index):
        return table_ref.at[:, pl.ds(pl.multiple_of(index * chunk, LANES), chunk)]

    def remote(src, dst, send, recv, device):
        return pltpu.make_async_remote_copy(
            src_ref=src,
            dst_ref=dst,
            send_sem=send,
            recv_sem=recv,
            device_id=device,
            device_id_type=MESH,
        )

    started = []
    arrive_table = {}
    arrive_rows = {}
    last = []
    for e in range(1, inner):
        copy = remote(
            table_piece(a), table_out.at[a, b], plane_send.at[0, e], plane_recv.at[0, e], plane(e)
        )
        copy.start()
        last.append(copy)
    for d in range(1, outer):
        copy = remote(
            table_piece(lax.rem(a + d, outer)),
            table_out.at[a, b],
            table_send.at[d],
            table_recv.at[d],
            column(d),
        )
        copy.start()
        arrive_table[d] = copy
    for f in range(1, cores):
        copy = remote(
            rows_ref, rows_out.at[a, core], core_send.at[0, f], core_recv.at[0, f], partner(f)
        )
        copy.start()
        last.append(copy)
    for d in range(1, outer):
        copy = remote(
            labels_ref, labels_out.at[a], label_send.at[d], label_recv.at[d], column(d)
        )
        copy.start()
        last.append(copy)
        copy = remote(
            rows_ref, rows_out.at[a, core], rows_send.at[d], rows_recv.at[d], column(d)
        )
        copy.start()
        arrive_rows[d] = copy
    local = [
        pltpu.make_async_copy(table_piece(a), table_out.at[a, b], local_sem.at[0]),
        pltpu.make_async_copy(rows_ref, rows_out.at[a, core], local_sem.at[1]),
        pltpu.make_async_copy(labels_ref, labels_out.at[a], local_sem.at[2]),
    ]
    for copy in local:
        copy.start()

    order = sorted(range(1, outer), key=lambda d: min(d, outer - d))
    for d in order:
        arrive_table[d].wait_recv()
        source = lax.rem(a + outer - d, outer)
        for e in range(1, inner):
            copy = remote(
                table_out.at[source, b],
                table_out.at[source, b],
                plane_send.at[d, e],
                plane_recv.at[d, e],
                plane(e),
            )
            copy.start()
            last.append(copy)
    for d in order:
        arrive_rows[d].wait_recv()
        source = lax.rem(a + outer - d, outer)
        for f in range(1, cores):
            copy = remote(
                rows_out.at[source, core],
                rows_out.at[source, core],
                core_send.at[d, f],
                core_recv.at[d, f],
                partner(f),
            )
            copy.start()
            last.append(copy)
    for copy in local:
        copy.wait()
    for d in order:
        arrive_table[d].wait_send()
        arrive_rows[d].wait_send()
    for copy in last:
        copy.wait()


def exchange(rows, labels, table, outer, inner, cores, chunk):
    any_space = pl.BlockSpec(memory_space=pl.ANY)
    dma = pltpu.SemaphoreType.DMA
    return pl.pallas_call(
        functools.partial(exchange_kernel, outer, inner, cores, chunk),
        out_shape=(
            jax.ShapeDtypeStruct((outer, cores) + rows.shape, rows.dtype),
            jax.ShapeDtypeStruct((outer,) + labels.shape, labels.dtype),
            jax.ShapeDtypeStruct((outer, inner, table.shape[0], chunk), table.dtype),
        ),
        in_specs=[any_space] * 3,
        out_specs=(any_space,) * 3,
        scratch_shapes=[
            dma((3,)),
            dma((outer,)),
            dma((outer,)),
            dma((outer, inner)),
            dma((outer, inner)),
            dma((outer,)),
            dma((outer,)),
            dma((outer, cores)),
            dma((outer, cores)),
            dma((outer,)),
            dma((outer,)),
        ],
        compiler_params=pltpu.CompilerParams(collective_id=0, has_side_effects=True),
    )(rows, labels, table)


def loss_kernel(block, shard_rows, limit_ref, rows_ref, labels_ref, table_ref, out_ref):
    rows = rows_ref[...]
    label = labels_ref[...]
    height = rows.shape[0]
    chunk = table_ref.shape[1]
    limit = limit_ref[0]
    start = limit_ref[1]
    top = jnp.full((height, 1), LOW, jnp.float32)
    total = jnp.zeros((height, 1), jnp.float32)
    picked = jnp.zeros((height, 1), jnp.float32)
    local_label = label - start
    for begin in range(0, chunk, block):
        logits = jnp.dot(
            rows, table_ref[:, begin : begin + block], preferred_element_type=jnp.float32
        )
        column = lax.broadcasted_iota(jnp.int32, (1, block), 1) + begin
        picked = picked + jnp.sum(
            jnp.where(column == local_label, logits, 0.0), axis=1, keepdims=True
        )
        logits = jnp.where(column < limit, logits, LOW)
        new_top = jnp.maximum(top, jnp.max(logits, axis=1, keepdims=True))
        total = total * jnp.exp(top - new_top) + jnp.sum(
            jnp.exp(logits - new_top), axis=1, keepdims=True
        )
        top = new_top
    total = jnp.where(label >= 0, total, 0.0)
    lane = lax.broadcasted_iota(jnp.int32, (height, LANES), 1)
    out_ref[...] = jnp.where(lane == 0, top, jnp.where(lane == 1, total, picked))


def partial_losses(rows, labels, table, limits, shard_rows):
    count, width = rows.shape
    chunk = table.shape[1]
    block = next(size for size in (1024, 512, 256, 128) if chunk % size == 0)
    height = 256
    return pl.pallas_call(
        functools.partial(loss_kernel, block, shard_rows),
        out_shape=jax.ShapeDtypeStruct((count, LANES), jnp.float32),
        grid=(count // height,),
        in_specs=[
            pl.BlockSpec(memory_space=pltpu.SMEM),
            pl.BlockSpec((height, width), lambda i: (i, 0)),
            pl.BlockSpec((height, 1), lambda i: (i, 0)),
            pl.BlockSpec((width, chunk), lambda i: (0, 0)),
        ],
        out_specs=pl.BlockSpec((height, LANES), lambda i: (i, 0)),
    )(limits, rows, labels, table)


def on_device(tokens, span_bounds, owner, decoder_states, norm_gain, embedding):
    seq_count, slot_count, local_width = decoder_states.shape
    owner_total = lax.axis_size("dp")
    cores = lax.axis_size("vocab")
    inner = INNER
    outer = owner_total // inner
    capacity = OWN_ROWS // owner_total
    shard_rows = embedding.shape[0]
    chunk = -(-shard_rows // (outer * LANES)) * LANES
    table = jnp.pad(embedding.T, ((0, 0), (0, outer * chunk - shard_rows)))

    slot_ids = jnp.arange(slot_count, dtype=jnp.int32)
    offsets = slot_ids % MAXSPAN
    starts = jnp.repeat(span_bounds[:, :, 0], MAXSPAN, axis=1)
    span_ends = jnp.repeat(span_bounds[:, :, 1], MAXSPAN, axis=1)
    is_live = (offsets[None, :] < span_ends - starts).reshape(-1)
    positions = jnp.minimum(starts + offsets[None, :], tokens.shape[1] - 1)
    here = positions[:, :, None] == jnp.arange(tokens.shape[1], dtype=jnp.int32)[None, None, :]
    labels = jnp.sum(jnp.where(here, tokens[:, None, :], 0), axis=2).reshape(-1)
    targets = owner.reshape(-1)
    slot_total = targets.shape[0]
    owner_hits = (targets[:, None] == jnp.arange(owner_total, dtype=jnp.int32)[None, :]).astype(
        jnp.bfloat16
    )
    device_slots = jnp.arange(slot_total, dtype=jnp.int32)
    earlier = (device_slots[:, None] > device_slots[None, :]).astype(jnp.bfloat16)
    running = jnp.dot(earlier, owner_hits, preferred_element_type=jnp.float32)
    slot_rank = jnp.sum(running * owner_hits.astype(jnp.float32), axis=1).astype(jnp.int32)
    target_row = targets * capacity + slot_rank
    placing = (target_row[None, :] == jnp.arange(OWN_ROWS, dtype=jnp.int32)[:, None]) & is_live[
        None, :
    ]
    sent_labels = jnp.sum(jnp.where(placing, labels[None, :] + 1, 0), axis=1) - 1
    onehot = placing.astype(jnp.bfloat16)
    states = decoder_states.reshape(slot_total, local_width)
    packed = jnp.dot(onehot, states, preferred_element_type=jnp.float32).astype(jnp.bfloat16)
    part = lax.all_to_all(packed, "vocab", split_axis=0, concat_axis=1, tiled=True)
    normed = normalize(part, norm_gain)

    label_tile = jnp.pad(sent_labels, (0, -OWN_ROWS % 1024)).reshape(-1, LANES)
    all_rows, all_labels, all_table = exchange(
        normed, label_tile, table, outer, inner, cores, chunk
    )
    rows = all_rows.reshape(outer * OWN_ROWS, -1)
    row_labels = all_labels.reshape(outer, -1)[:, :OWN_ROWS].reshape(-1, 1)
    full_table = all_table.reshape(rows.shape[1], chunk)
    first = lax.axis_index("dp") // inner * chunk
    limits = jnp.stack(
        [shard_rows - first, lax.axis_index("vocab") * shard_rows + first]
    ).astype(jnp.int32)
    out_of_range = row_labels - limits[1] >= limits[0]
    kept = jnp.where(out_of_range, shard_rows * cores + limits[1] + chunk, row_labels)
    partial = partial_losses(rows, kept, full_table, limits, shard_rows)

    values = partial[:, :3].reshape(outer, owner_total, capacity * 3)
    values = jnp.swapaxes(values, 0, 1).reshape(owner_total, 1, outer * capacity * 3)
    values = jnp.broadcast_to(values, (owner_total, cores, outer * capacity * 3))
    values = values.reshape(owner_total * cores, outer * capacity * 3)
    landed = lax.all_to_all(values, ("dp", "vocab"), split_axis=0, concat_axis=0, tiled=True)
    landed = landed.reshape(outer, inner, cores, outer, capacity, 3)
    tops, totals, picks = landed[..., 0], landed[..., 1], landed[..., 2]
    row_top = jnp.max(tops, axis=(0, 2))
    exp_total = jnp.sum(totals * jnp.exp(tops - row_top[None, :, None]), axis=(0, 2))
    label_logit = jnp.sum(picks, axis=(0, 2))
    row_loss = row_top + jnp.log(jnp.where(exp_total > 0.0, exp_total, 1.0)) - label_logit
    losses = jnp.where(exp_total > 0.0, row_loss, 0.0)
    return jnp.swapaxes(losses, 0, 1).reshape(-1)


def solution(mesh):
    placed = (
        P("dp", None),
        P("dp", None, None),
        P("dp", None, None),
        P("dp", None, "vocab"),
        P(),
        P("vocab", "dp"),
    )
    return jax.shard_map(on_device, mesh=mesh, in_specs=placed, out_specs=P("dp"), check_vma=False)
```

```python
import functools

import jax
import jax.numpy as jnp
from jax import lax
from jax.experimental import pallas as pl
from jax.experimental.pallas import tpu as pltpu
from jax.sharding import PartitionSpec as P

MAXSPAN = 5
OWN_ROWS = 768
INNER = 4
LANES = 128
LOW = -1e30
MESH = pl.DeviceIdType.MESH


epsilon = 1e-06


def normalize(rows, norm_gain):
    values = rows.astype(jnp.float32)
    mean_square = jnp.mean(values * values, axis=1, keepdims=True)
    scaled = (
        values
        * lax.rsqrt(mean_square + epsilon)
        * norm_gain.astype(jnp.float32)
        * values.shape[1] ** (-0.5)
    )
    return scaled.astype(jnp.bfloat16)


def exchange_loss_kernel(
    outer,
    inner,
    cores,
    chunk,
    block,
    limit,
    rows_ref,
    labels_ref,
    table_ref,
    out_ref,
    rows_vm,
    labels_vm,
    table_vm,
    stat_vm,
    local_sem,
    column_send,
    column_recv,
    ring_send,
    ring_recv,
    rows_send,
    rows_recv,
    core_send,
    core_recv,
    label_send,
    label_recv,
):
    dp = lax.axis_index("dp")
    core = lax.axis_index("vocab")
    a = dp // inner
    b = lax.rem(dp, inner)
    width = table_ref.shape[0]
    part = rows_ref.shape[0]
    per_source = part * cores
    stages = chunk // block

    def gray(p):
        return p + (p // 2) * (1 - 2 * lax.rem(p, 2))

    spot = gray(b)
    b_next = gray(lax.rem(spot + 1, inner))
    b_far = gray(lax.rem(spot + 2, inner))
    b_prev = gray(lax.rem(spot + inner - 1, inner))
    next_device = (a * inner + b_next, core)
    prev_device = (a * inner + b_prev, core)

    def column(d):
        return (lax.rem(a + d, outer) * inner + b, core)

    def partner(f):
        return (dp, lax.rem(core + f, cores))

    barrier = pltpu.get_barrier_semaphore()
    greeted = (
        [column(d) for d in range(1, outer)]
        + [next_device, prev_device]
        + [partner(f) for f in range(1, cores)]
    )
    for device in greeted:
        pl.semaphore_signal(barrier, inc=1, device_id=device, device_id_type=MESH)
    pl.semaphore_wait(barrier, len(greeted))

    def remote(src, dst, send, recv, device):
        return pltpu.make_async_remote_copy(
            src_ref=src,
            dst_ref=dst,
            send_sem=send,
            recv_sem=recv,
            device_id=device,
            device_id_type=MESH,
        )

    def origin(index, stage):
        return table_ref.at[
            :, pl.ds(pl.multiple_of(index * chunk + stage * block, LANES), block)
        ]

    def landed(row, col, stage):
        return table_vm.at[
            pl.ds(pl.multiple_of((row * inner + col) * width, width), width),
            pl.ds(stage * block, block),
        ]

    def behind(d):
        return lax.rem(a + outer - d, outer)

    def column_copy(d, s):
        return remote(
            origin(lax.rem(a + d, outer), s),
            landed(a, b, s),
            column_send.at[d, s],
            column_recv.at[d, s],
            column(d),
        )

    def ring_copy(kind, d, s):
        held_from = b if kind < 2 else (b_prev if kind == 2 else b_next)
        place = landed(behind(d), held_from, s)
        return remote(
            origin(a, s) if d == 0 and kind < 2 else place,
            place,
            ring_send.at[kind, d, s],
            ring_recv.at[kind, d, s],
            next_device if kind % 2 == 0 else prev_device,
        )

    def row_slot(source):
        return rows_vm.at[pl.ds(pl.multiple_of(source * per_source + core * part, 16), part), :]

    def row_copy(side, dist):
        source = a - dist if side == 0 else a + dist
        device = ((a + 1 if side == 0 else a - 1) * inner + b, core)
        return remote(
            rows_ref if dist == 0 else row_slot(source),
            row_slot(source),
            rows_send.at[side, dist],
            rows_recv.at[side, dist],
            device,
        )

    def core_copy(side, dist, f):
        source = a - dist if side == 0 else a + dist
        return remote(
            rows_ref if dist == 0 else row_slot(source),
            row_slot(source),
            core_send.at[side, dist, f],
            core_recv.at[side, dist, f],
            partner(f),
        )

    def label_copy(d):
        return remote(
            labels_ref, labels_vm.at[a], label_send.at[d], label_recv.at[d], column(d)
        )

    def has(side, dist):
        return a - dist >= 0 if side == 0 else a + dist < outer

    def goes_on(side):
        return a + 1 < outer if side == 0 else a >= 1

    def send_stage(s):
        for d in range(1, outer):
            column_copy(d, s).start()

    def ring_first(s):
        for d in range(1, outer):
            column_copy(d, s).wait_recv()
            for kind in (0, 1):
                ring_copy(kind, d, s).start()

    def ring_second(s):
        for d in range(outer):
            kind = d % 2
            ring_copy(kind, d, s).wait_recv()
            ring_copy(kind + 2, d, s).start()

    def ring_finish(s):
        for d in range(outer):
            ring_copy(1 - d % 2, d, s).wait_recv()
            ring_copy(d % 2 + 2, d, s).wait_recv()

    def row_arrive(dist):
        for side in (0, 1):

            @pl.when(has(side, dist))
            def _():
                row_copy(side, dist - 1).wait_recv()

                @pl.when(goes_on(side))
                def _():
                    row_copy(side, dist).start()

                for f in range(1, cores):
                    core_copy(side, dist, f).start()

    def row_finish(dist):
        for side in (0, 1):

            @pl.when(has(side, dist))
            def _():
                for f in range(1, cores):
                    core_copy(side, dist, f).wait_recv()

    local = [
        pltpu.make_async_copy(rows_ref, row_slot(a), local_sem.at[0]),
        pltpu.make_async_copy(labels_ref, labels_vm.at[a], local_sem.at[1]),
    ] + [
        pltpu.make_async_copy(origin(a, s), landed(a, b, s), local_sem.at[2 + s])
        for s in range(stages)
    ]
    early = min(2, stages)
    for s in range(early):
        send_stage(s)
    for d in range(1, outer):
        label_copy(d).start()
    for f in range(1, cores):
        core_copy(0, 0, f).start()
    for side in (0, 1):

        @pl.when(goes_on(side))
        def _():
            row_copy(side, 0).start()

    for s in range(early, stages):
        send_stage(s)
    for s in range(stages):
        for kind in (0, 1):
            if s < early:
                ring_copy(kind, 0, s).start()
    for copy in local:
        copy.start()

    eye = lax.broadcasted_iota(jnp.int32, (LANES, LANES), 0) == lax.broadcasted_iota(
        jnp.int32, (LANES, LANES), 1
    )
    height = 2 * LANES
    lane = lax.broadcasted_iota(jnp.int32, (height, LANES), 1)

    @pl.loop(0, stat_vm.shape[0] // height)
    def _(i):
        stat_vm[pl.ds(pl.multiple_of(i * height, height), height), :] = jnp.where(
            lane == 0, LOW, 0.0
        )

    first = a * chunk
    shift = core * limit + first

    def tile(source, begin, index):
        at = pl.ds(pl.multiple_of(source * per_source + index * height, height), height)
        wide = labels_vm[source, pl.ds(2 * index, 2), :]
        label = jnp.concatenate(
            [
                jnp.sum(jnp.where(eye, wide[h : h + 1, :], 0), axis=1, keepdims=True)
                for h in range(2)
            ],
            axis=0,
        )
        logits = jnp.dot(
            rows_vm[at, :],
            table_vm[:, pl.ds(begin, block)],
            preferred_element_type=jnp.float32,
        )
        col = lax.broadcasted_iota(jnp.int32, (1, block), 1) + begin
        stat = stat_vm[at, :]
        top, total, picked = stat[:, 0:1], stat[:, 1:2], stat[:, 2:3]
        inside = col + first < limit
        wanted = jnp.where(inside, col + shift, -2)
        picked = picked + jnp.sum(jnp.where(wanted == label, logits, 0.0), axis=1, keepdims=True)
        logits = jnp.where(inside, logits, LOW)
        new_top = jnp.maximum(top, jnp.max(logits, axis=1, keepdims=True))
        total = total * jnp.exp(top - new_top) + jnp.sum(
            jnp.exp(logits - new_top), axis=1, keepdims=True
        )
        total = jnp.where(label >= 0, total, 0.0)
        stat_vm[at, :] = jnp.where(lane == 0, new_top, jnp.where(lane == 1, total, picked))

    def compute(dist, low, high):
        @pl.loop(0, 1 if dist == 0 else 2)
        def _(side):
            source = a + (2 * side - 1) * dist

            @pl.when((source >= 0) & (source < outer))
            def _():
                @pl.loop(low, high)
                def _(s):
                    begin = pl.multiple_of(s * block, block)

                    @pl.loop(0, per_source // height)
                    def _(index):
                        tile(source, begin, index)

    for s in range(early):
        ring_first(s)
        if s == 0:
            ring_second(0)
    for copy in local:
        copy.wait()
    for f in range(1, cores):
        core_copy(0, 0, f).wait_recv()
    for d in range(1, outer):
        label_copy(d).wait_recv()
    ring_finish(0)
    done = [0] * outer
    reached = 1

    def catch_up(full):
        for dist in range(reached):
            if done[dist] < full:
                compute(dist, done[dist], full)
                done[dist] = full

    catch_up(1)
    row_arrive(1)
    reached = 2
    if stages > 1:
        ring_second(1)
    for s in range(early, stages):
        for kind in (0, 1):
            ring_copy(kind, 0, s).start()
    if stages > 2:
        ring_first(2)
    row_finish(1)
    if stages > 1:
        ring_finish(1)
    catch_up(min(2, stages))
    for s in range(2, stages):
        if s + 1 < stages:
            ring_first(s + 1)
        ring_second(s)
        if reached < outer and s > 2:
            row_arrive(reached)
            row_finish(reached)
            catch_up(s)
            reached += 1
            catch_up(s)
        ring_finish(s)
        catch_up(s + 1)
    while reached < outer:
        row_arrive(reached)
        row_finish(reached)
        reached += 1
        catch_up(stages)

    @pl.loop(0, outer * per_source // LANES)
    def _(i):
        stat = stat_vm[pl.ds(pl.multiple_of(i * LANES, LANES), LANES), :]
        for k in range(3):
            out_ref[k, pl.ds(i, 1), :] = jnp.sum(
                jnp.where(eye, stat[:, k : k + 1], 0.0), axis=0, keepdims=True
            )

    for s in range(stages):
        for d in range(1, outer):
            column_copy(d, s).wait_send()
        for d in range(outer):
            for kind in (0, 1, d % 2 + 2):
                ring_copy(kind, d, s).wait_send()
    for d in range(1, outer):
        label_copy(d).wait_send()
    for f in range(1, cores):
        core_copy(0, 0, f).wait_send()
    for side in (0, 1):

        @pl.when(goes_on(side))
        def _():
            row_copy(side, 0).wait_send()

        for dist in range(1, outer):

            @pl.when(has(side, dist))
            def _():
                @pl.when(goes_on(side))
                def _():
                    row_copy(side, dist).wait_send()

                for f in range(1, cores):
                    core_copy(side, dist, f).wait_send()


def partial_losses(rows, labels, table, outer, inner, cores, chunk, limit):
    block = next(size for size in (1024, 512, 256, 128) if chunk % size == 0)
    stages = chunk // block
    any_space = pl.BlockSpec(memory_space=pl.ANY)
    dma = pltpu.SemaphoreType.DMA
    count = outer * cores * rows.shape[0]
    width = rows.shape[1]
    return pl.pallas_call(
        functools.partial(exchange_loss_kernel, outer, inner, cores, chunk, block, limit),
        out_shape=jax.ShapeDtypeStruct((3, count // LANES, LANES), jnp.float32),
        in_specs=[any_space] * 3,
        out_specs=pl.BlockSpec(memory_space=pltpu.VMEM),
        scratch_shapes=[
            pltpu.VMEM((count, width), rows.dtype),
            pltpu.VMEM((outer,) + labels.shape, labels.dtype),
            pltpu.VMEM((width, chunk), table.dtype),
            pltpu.VMEM((count, LANES), jnp.float32),
            dma((2 + stages,)),
            dma((outer, stages)),
            dma((outer, stages)),
            dma((4, outer, stages)),
            dma((4, outer, stages)),
            dma((2, outer)),
            dma((2, outer)),
            dma((2, outer, cores)),
            dma((2, outer, cores)),
            dma((outer,)),
            dma((outer,)),
        ],
        compiler_params=pltpu.CompilerParams(collective_id=0, has_side_effects=True),
    )(rows, labels, table)


def on_device(tokens, span_bounds, owner, decoder_states, norm_gain, embedding):
    seq_count, slot_count, local_width = decoder_states.shape
    owner_total = lax.axis_size("dp")
    cores = lax.axis_size("vocab")
    inner = INNER
    outer = owner_total // inner
    capacity = OWN_ROWS // owner_total
    shard_rows = embedding.shape[0]
    chunk = -(-shard_rows // (outer * LANES)) * LANES
    table = jnp.pad(embedding.T, ((0, 0), (0, outer * chunk - shard_rows)))

    slot_ids = jnp.arange(slot_count, dtype=jnp.int32)
    offsets = slot_ids % MAXSPAN
    starts = jnp.repeat(span_bounds[:, :, 0], MAXSPAN, axis=1)
    span_ends = jnp.repeat(span_bounds[:, :, 1], MAXSPAN, axis=1)
    is_live = (offsets[None, :] < span_ends - starts).reshape(-1)
    positions = jnp.minimum(starts + offsets[None, :], tokens.shape[1] - 1)
    here = positions[:, :, None] == jnp.arange(tokens.shape[1], dtype=jnp.int32)[None, None, :]
    labels = jnp.sum(jnp.where(here, tokens[:, None, :], 0), axis=2).reshape(-1)
    targets = owner.reshape(-1)
    slot_total = targets.shape[0]
    owner_hits = (targets[:, None] == jnp.arange(owner_total, dtype=jnp.int32)[None, :]).astype(
        jnp.bfloat16
    )
    device_slots = jnp.arange(slot_total, dtype=jnp.int32)
    earlier = (device_slots[:, None] > device_slots[None, :]).astype(jnp.bfloat16)
    running = jnp.dot(earlier, owner_hits, preferred_element_type=jnp.float32)
    slot_rank = jnp.sum(running * owner_hits.astype(jnp.float32), axis=1).astype(jnp.int32)
    target_row = targets * capacity + slot_rank
    placing = (target_row[None, :] == jnp.arange(OWN_ROWS, dtype=jnp.int32)[:, None]) & is_live[
        None, :
    ]
    sent_labels = jnp.sum(jnp.where(placing, labels[None, :] + 1, 0), axis=1) - 1
    onehot = placing.astype(jnp.bfloat16)
    states = decoder_states.reshape(slot_total, local_width)
    packed = jnp.dot(onehot, states, preferred_element_type=jnp.float32).astype(jnp.bfloat16)
    part = lax.all_to_all(packed, "vocab", split_axis=0, concat_axis=1, tiled=True)
    normed = normalize(part, norm_gain)

    label_tile = jnp.pad(sent_labels, (0, -OWN_ROWS % 1024)).reshape(-1, LANES)
    partial = partial_losses(
        normed, label_tile, table, outer, inner, cores, chunk, shard_rows
    )

    size = 3 * outer * capacity
    values = partial.reshape(3, outer, owner_total, capacity)
    values = values.transpose(2, 0, 1, 3).reshape(owner_total, 1, size)
    values = jnp.broadcast_to(values, (owner_total, cores, size))
    values = values.reshape(owner_total * cores, size)
    landed = lax.all_to_all(values, ("dp", "vocab"), split_axis=0, concat_axis=0, tiled=True)
    landed = landed.reshape(outer, inner, cores, 3, outer, capacity)
    tops, totals, picks = landed[:, :, :, 0], landed[:, :, :, 1], landed[:, :, :, 2]
    row_top = jnp.max(tops, axis=(0, 2))
    exp_total = jnp.sum(totals * jnp.exp(tops - row_top[None, :, None]), axis=(0, 2))
    label_logit = jnp.sum(picks, axis=(0, 2))
    row_loss = row_top + jnp.log(jnp.where(exp_total > 0.0, exp_total, 1.0)) - label_logit
    losses = jnp.where(exp_total > 0.0, row_loss, 0.0)
    return jnp.swapaxes(losses, 0, 1).reshape(-1)


def solution(mesh):
    placed = (
        P("dp", None),
        P("dp", None, None),
        P("dp", None, None),
        P("dp", None, "vocab"),
        P(),
        P("vocab", "dp"),
    )
    return jax.shard_map(on_device, mesh=mesh, in_specs=placed, out_specs=P("dp"), check_vma=False)
```

```python
import functools

import jax
import jax.numpy as jnp
from jax import lax
from jax.experimental import pallas as pl
from jax.experimental.pallas import tpu as pltpu
from jax.sharding import PartitionSpec as P

MAXSPAN = 5
OWN_ROWS = 768
INNER = 4
LANES = 128
LOW = -1e30
MESH = pl.DeviceIdType.MESH


epsilon = 1e-06


def normalize(rows, norm_gain):
    values = rows.astype(jnp.float32)
    mean_square = jnp.mean(values * values, axis=1, keepdims=True)
    scaled = (
        values
        * lax.rsqrt(mean_square + epsilon)
        * norm_gain.astype(jnp.float32)
        * values.shape[1] ** (-0.5)
    )
    return scaled.astype(jnp.bfloat16)


def exchange_loss_kernel(
    outer,
    inner,
    cores,
    chunk,
    block,
    limit,
    rows_ref,
    labels_ref,
    table_ref,
    out_ref,
    rows_vm,
    labels_vm,
    table_vm,
    stat_vm,
    local_sem,
    column_send,
    column_recv,
    ring_send,
    ring_recv,
    rows_send,
    rows_recv,
    core_send,
    core_recv,
    label_send,
    label_recv,
):
    dp = lax.axis_index("dp")
    core = lax.axis_index("vocab")
    a = dp // inner
    b = lax.rem(dp, inner)
    width = table_ref.shape[0]
    part = rows_ref.shape[0]
    per_source = part * cores
    stages = chunk // block

    def gray(p):
        return p + (p // 2) * (1 - 2 * lax.rem(p, 2))

    spot = gray(b)
    b_next = gray(lax.rem(spot + 1, inner))
    b_far = gray(lax.rem(spot + 2, inner))
    b_prev = gray(lax.rem(spot + inner - 1, inner))
    next_device = (a * inner + b_next, core)
    prev_device = (a * inner + b_prev, core)

    def column(d):
        return (lax.rem(a + d, outer) * inner + b, core)

    def partner(f):
        return (dp, lax.rem(core + f, cores))

    barrier = pltpu.get_barrier_semaphore()
    greeted = (
        [column(d) for d in range(1, outer)]
        + [next_device, prev_device]
        + [partner(f) for f in range(1, cores)]
    )
    for device in greeted:
        pl.semaphore_signal(barrier, inc=1, device_id=device, device_id_type=MESH)
    pl.semaphore_wait(barrier, len(greeted))

    def remote(src, dst, send, recv, device):
        return pltpu.make_async_remote_copy(
            src_ref=src,
            dst_ref=dst,
            send_sem=send,
            recv_sem=recv,
            device_id=device,
            device_id_type=MESH,
        )

    def origin(index, stage):
        return table_ref.at[
            :, pl.ds(pl.multiple_of(index * chunk + stage * block, LANES), block)
        ]

    def landed(row, col, stage):
        return table_vm.at[
            pl.ds(pl.multiple_of((row * inner + col) * width, width), width),
            pl.ds(stage * block, block),
        ]

    def behind(d):
        return lax.rem(a + outer - d, outer)

    def column_copy(d, s):
        return remote(
            origin(lax.rem(a + d, outer), s),
            landed(a, b, s),
            column_send.at[d, s],
            column_recv.at[d, s],
            column(d),
        )

    def ring_copy(kind, d, s):
        held_from = b if kind < 2 else (b_prev if kind == 2 else b_next)
        place = landed(behind(d), held_from, s)
        return remote(
            origin(a, s) if d == 0 and kind < 2 else place,
            place,
            ring_send.at[kind, d, s],
            ring_recv.at[kind, d, s],
            next_device if kind % 2 == 0 else prev_device,
        )

    def row_slot(source):
        return rows_vm.at[pl.ds(pl.multiple_of(source * per_source + core * part, 16), part), :]

    def row_copy(side, dist):
        source = a - dist if side == 0 else a + dist
        device = ((a + 1 if side == 0 else a - 1) * inner + b, core)
        return remote(
            rows_ref if dist == 0 else row_slot(source),
            row_slot(source),
            rows_send.at[side, dist],
            rows_recv.at[side, dist],
            device,
        )

    def core_copy(side, dist, f):
        source = a - dist if side == 0 else a + dist
        return remote(
            rows_ref if dist == 0 else row_slot(source),
            row_slot(source),
            core_send.at[side, dist, f],
            core_recv.at[side, dist, f],
            partner(f),
        )

    def label_copy(d):
        return remote(
            labels_ref, labels_vm.at[a], label_send.at[d], label_recv.at[d], column(d)
        )

    def has(side, dist):
        return a - dist >= 0 if side == 0 else a + dist < outer

    def goes_on(side):
        return a + 1 < outer if side == 0 else a >= 1

    def send_stage(s):
        for d in range(1, outer):
            column_copy(d, s).start()

    def ring_first(s):
        for d in range(1, outer):
            column_copy(d, s).wait_recv()
            for kind in (0, 1):
                ring_copy(kind, d, s).start()

    def ring_second(s):
        for d in range(outer):
            kind = d % 2
            ring_copy(kind, d, s).wait_recv()
            ring_copy(kind + 2, d, s).start()

    def ring_finish(s):
        for d in range(outer):
            ring_copy(1 - d % 2, d, s).wait_recv()
            ring_copy(d % 2 + 2, d, s).wait_recv()

    def row_arrive(dist):
        for side in (0, 1):

            @pl.when(has(side, dist))
            def _():
                row_copy(side, dist - 1).wait_recv()

                @pl.when(goes_on(side))
                def _():
                    row_copy(side, dist).start()

                for f in range(1, cores):
                    core_copy(side, dist, f).start()

    def row_finish(dist):
        for side in (0, 1):

            @pl.when(has(side, dist))
            def _():
                for f in range(1, cores):
                    core_copy(side, dist, f).wait_recv()

    local = [
        pltpu.make_async_copy(rows_ref, row_slot(a), local_sem.at[0]),
        pltpu.make_async_copy(labels_ref, labels_vm.at[a], local_sem.at[1]),
    ] + [
        pltpu.make_async_copy(origin(a, s), landed(a, b, s), local_sem.at[2 + s])
        for s in range(stages)
    ]
    early = min(2, stages)
    for s in range(early):
        send_stage(s)
    for d in range(1, outer):
        label_copy(d).start()
    for f in range(1, cores):
        core_copy(0, 0, f).start()
    for side in (0, 1):

        @pl.when(goes_on(side))
        def _():
            row_copy(side, 0).start()

    for s in range(early, stages):
        send_stage(s)
    for s in range(stages):
        for kind in (0, 1):
            if s < early:
                ring_copy(kind, 0, s).start()
    for copy in local:
        copy.start()

    eye = lax.broadcasted_iota(jnp.int32, (LANES, LANES), 0) == lax.broadcasted_iota(
        jnp.int32, (LANES, LANES), 1
    )
    height = 2 * LANES
    lane = lax.broadcasted_iota(jnp.int32, (1, LANES), 1)

    @pl.loop(0, stat_vm.shape[1] // height)
    def _(i):
        at = pl.ds(pl.multiple_of(i * height, height), height)
        stat_vm[0, at, :] = jnp.full((height, LANES), LOW, jnp.float32)
        stat_vm[1, at, :] = jnp.zeros((height, LANES), jnp.float32)
        stat_vm[2, at, :] = jnp.zeros((height, LANES), jnp.float32)

    first = a * chunk
    shift = core * limit + first

    def tile(source, begin, index):
        at = pl.ds(pl.multiple_of(source * per_source + index * height, height), height)
        wide = labels_vm[source, pl.ds(2 * index, 2), :]
        label = jnp.concatenate(
            [
                jnp.sum(jnp.where(eye, wide[h : h + 1, :], 0), axis=1, keepdims=True)
                for h in range(2)
            ],
            axis=0,
        )
        logits = jnp.dot(
            rows_vm[at, :],
            table_vm[:, pl.ds(begin, block)],
            preferred_element_type=jnp.float32,
        )
        label = jnp.broadcast_to(label, (height, LANES))
        top, total, picked = stat_vm[0, at, :], stat_vm[1, at, :], stat_vm[2, at, :]
        new_top = top
        pieces = []
        for start in range(0, block, LANES):
            piece = logits[:, start : start + LANES]
            col = lane + (begin + start)
            inside = col + first < limit
            wanted = jnp.where(inside, col + shift, -2)
            picked = picked + jnp.where(wanted == label, piece, 0.0)
            piece = jnp.where(inside, piece, LOW)
            new_top = jnp.maximum(new_top, piece)
            pieces.append(piece)
        total = total * jnp.exp(top - new_top)
        for piece in pieces:
            total = total + jnp.exp(piece - new_top)
        stat_vm[0, at, :] = new_top
        stat_vm[1, at, :] = total
        stat_vm[2, at, :] = picked

    def compute(dist, low, high):
        @pl.loop(0, 1 if dist == 0 else 2)
        def _(side):
            source = a + (2 * side - 1) * dist

            @pl.when((source >= 0) & (source < outer))
            def _():
                @pl.loop(low, high)
                def _(s):
                    begin = pl.multiple_of(s * block, block)

                    @pl.loop(0, per_source // height, unroll=True)
                    def _(index):
                        tile(source, begin, index)

    for s in range(early):
        ring_first(s)
        if s == 0:
            ring_second(0)
    for copy in local:
        copy.wait()
    for f in range(1, cores):
        core_copy(0, 0, f).wait_recv()
    for d in range(1, outer):
        label_copy(d).wait_recv()
    ring_finish(0)
    done = [0] * outer
    reached = 1

    def catch_up(full):
        for dist in range(reached):
            if done[dist] < full:
                compute(dist, done[dist], full)
                done[dist] = full

    catch_up(1)
    row_arrive(1)
    reached = 2
    if stages > 1:
        ring_second(1)
    for s in range(early, stages):
        for kind in (0, 1):
            ring_copy(kind, 0, s).start()
    if stages > 2:
        ring_first(2)
    row_finish(1)
    if stages > 1:
        ring_finish(1)
    catch_up(min(2, stages))
    for s in range(2, stages):
        if s + 1 < stages:
            ring_first(s + 1)
        ring_second(s)
        if reached < outer and s > 2:
            row_arrive(reached)
            row_finish(reached)
            catch_up(s)
            reached += 1
            catch_up(s)
        ring_finish(s)
        catch_up(s + 1)
    while reached < outer:
        row_arrive(reached)
        row_finish(reached)
        reached += 1
        catch_up(stages)

    groups = per_source // LANES

    @pl.loop(0, outer * groups)
    def _(i):
        at = pl.ds(pl.multiple_of(i * LANES, LANES), LANES)
        top = jnp.max(stat_vm[0, at, :], axis=1, keepdims=True)
        total = jnp.sum(stat_vm[1, at, :] * jnp.exp(stat_vm[0, at, :] - top), axis=1, keepdims=True)
        picked = jnp.sum(stat_vm[2, at, :], axis=1, keepdims=True)
        live = labels_vm[i // groups, pl.ds(lax.rem(i, groups), 1), :] >= 0
        for k, value in enumerate((top, total, picked)):
            row = jnp.sum(jnp.where(eye, value, 0.0), axis=0, keepdims=True)
            out_ref[k, pl.ds(i, 1), :] = jnp.where(live, row, 0.0) if k == 1 else row

    for s in range(stages):
        for d in range(1, outer):
            column_copy(d, s).wait_send()
        for d in range(outer):
            for kind in (0, 1, d % 2 + 2):
                ring_copy(kind, d, s).wait_send()
    for d in range(1, outer):
        label_copy(d).wait_send()
    for f in range(1, cores):
        core_copy(0, 0, f).wait_send()
    for side in (0, 1):

        @pl.when(goes_on(side))
        def _():
            row_copy(side, 0).wait_send()

        for dist in range(1, outer):

            @pl.when(has(side, dist))
            def _():
                @pl.when(goes_on(side))
                def _():
                    row_copy(side, dist).wait_send()

                for f in range(1, cores):
                    core_copy(side, dist, f).wait_send()


def partial_losses(rows, labels, table, outer, inner, cores, chunk, limit):
    block = next(size for size in (1024, 512, 256, 128) if chunk % size == 0)
    stages = chunk // block
    any_space = pl.BlockSpec(memory_space=pl.ANY)
    dma = pltpu.SemaphoreType.DMA
    count = outer * cores * rows.shape[0]
    width = rows.shape[1]
    return pl.pallas_call(
        functools.partial(exchange_loss_kernel, outer, inner, cores, chunk, block, limit),
        out_shape=jax.ShapeDtypeStruct((3, count // LANES, LANES), jnp.float32),
        in_specs=[any_space] * 3,
        out_specs=pl.BlockSpec(memory_space=pltpu.VMEM),
        scratch_shapes=[
            pltpu.VMEM((count, width), rows.dtype),
            pltpu.VMEM((outer,) + labels.shape, labels.dtype),
            pltpu.VMEM((width, chunk), table.dtype),
            pltpu.VMEM((3, count, LANES), jnp.float32),
            dma((2 + stages,)),
            dma((outer, stages)),
            dma((outer, stages)),
            dma((4, outer, stages)),
            dma((4, outer, stages)),
            dma((2, outer)),
            dma((2, outer)),
            dma((2, outer, cores)),
            dma((2, outer, cores)),
            dma((outer,)),
            dma((outer,)),
        ],
        compiler_params=pltpu.CompilerParams(collective_id=0, has_side_effects=True),
    )(rows, labels, table)


def on_device(tokens, span_bounds, owner, decoder_states, norm_gain, embedding):
    seq_count, slot_count, local_width = decoder_states.shape
    owner_total = lax.axis_size("dp")
    cores = lax.axis_size("vocab")
    inner = INNER
    outer = owner_total // inner
    capacity = OWN_ROWS // owner_total
    shard_rows = embedding.shape[0]
    chunk = -(-shard_rows // (outer * LANES)) * LANES
    table = jnp.pad(embedding.T, ((0, 0), (0, outer * chunk - shard_rows)))

    slot_ids = jnp.arange(slot_count, dtype=jnp.int32)
    offsets = slot_ids % MAXSPAN
    starts = jnp.repeat(span_bounds[:, :, 0], MAXSPAN, axis=1)
    span_ends = jnp.repeat(span_bounds[:, :, 1], MAXSPAN, axis=1)
    is_live = (offsets[None, :] < span_ends - starts).reshape(-1)
    positions = jnp.minimum(starts + offsets[None, :], tokens.shape[1] - 1)
    here = positions[:, :, None] == jnp.arange(tokens.shape[1], dtype=jnp.int32)[None, None, :]
    labels = jnp.sum(jnp.where(here, tokens[:, None, :], 0), axis=2).reshape(-1)
    targets = owner.reshape(-1)
    slot_total = targets.shape[0]
    owner_hits = (targets[:, None] == jnp.arange(owner_total, dtype=jnp.int32)[None, :]).astype(
        jnp.bfloat16
    )
    device_slots = jnp.arange(slot_total, dtype=jnp.int32)
    earlier = (device_slots[:, None] > device_slots[None, :]).astype(jnp.bfloat16)
    running = jnp.dot(earlier, owner_hits, preferred_element_type=jnp.float32)
    slot_rank = jnp.sum(running * owner_hits.astype(jnp.float32), axis=1).astype(jnp.int32)
    target_row = targets * capacity + slot_rank
    placing = (target_row[None, :] == jnp.arange(OWN_ROWS, dtype=jnp.int32)[:, None]) & is_live[
        None, :
    ]
    sent_labels = jnp.sum(jnp.where(placing, labels[None, :] + 1, 0), axis=1) - 1
    onehot = placing.astype(jnp.bfloat16)
    states = decoder_states.reshape(slot_total, local_width)
    packed = jnp.dot(onehot, states, preferred_element_type=jnp.float32).astype(jnp.bfloat16)
    part = lax.all_to_all(packed, "vocab", split_axis=0, concat_axis=1, tiled=True)
    normed = normalize(part, norm_gain)

    label_tile = jnp.pad(sent_labels, (0, -OWN_ROWS % 1024)).reshape(-1, LANES)
    partial = partial_losses(
        normed, label_tile, table, outer, inner, cores, chunk, shard_rows
    )

    size = 3 * outer * capacity
    values = partial.reshape(3, outer, owner_total, capacity)
    values = values.transpose(2, 0, 1, 3).reshape(owner_total, 1, size)
    values = jnp.broadcast_to(values, (owner_total, cores, size))
    values = values.reshape(owner_total * cores, size)
    landed = lax.all_to_all(values, ("dp", "vocab"), split_axis=0, concat_axis=0, tiled=True)
    landed = landed.reshape(outer, inner, cores, 3, outer, capacity)
    tops, totals, picks = landed[:, :, :, 0], landed[:, :, :, 1], landed[:, :, :, 2]
    row_top = jnp.max(tops, axis=(0, 2))
    exp_total = jnp.sum(totals * jnp.exp(tops - row_top[None, :, None]), axis=(0, 2))
    label_logit = jnp.sum(picks, axis=(0, 2))
    row_loss = row_top + jnp.log(jnp.where(exp_total > 0.0, exp_total, 1.0)) - label_logit
    losses = jnp.where(exp_total > 0.0, row_loss, 0.0)
    return jnp.swapaxes(losses, 0, 1).reshape(-1)


def solution(mesh):
    placed = (
        P("dp", None),
        P("dp", None, None),
        P("dp", None, None),
        P("dp", None, "vocab"),
        P(),
        P("vocab", "dp"),
    )
    return jax.shard_map(on_device, mesh=mesh, in_specs=placed, out_specs=P("dp"), check_vma=False)
```
